32 devices in a mesh: sector: 8 (over z, core), term: 4 (over y, x).
Axes of the slice: x: 2, y: 2, z: 4, core: 2. Of those that a mesh axis runs over, the one named last changes fastest.
Arguments:
- psi: bfloat16 [128, 256, 256], P('sector'), may hold values from -6 to 6
- sector_sizes: int32 [128], P('sector'), may hold values from 64 to 256, as said below
- left_env: bfloat16 [192, 8, 256, 256], P('term', 'sector'), may hold values from -0.109375 to 0.109375
- right_env: bfloat16 [192, 8, 256, 256], P('term', 'sector'), may hold values from -0.375 to 0.375
- target: int32 [192, 8], P('term', 'sector'), may hold values from 0 to 127, as said below
- source: int32 [192, 8], P('term', 'sector'), may hold values from 0 to 127, as said below
- live_count: int32 [4, 8], P('term', 'sector'), may hold values from 1 to 48, as said below
Outputs:
- sigma: float32 [128, 256, 256], P('sector', 'term')
The draws below stay inside these ranges and needn't reach their ends.
Inputs may be any that keep to these rules, and one draw needn't show every extreme that they name: target[j, g] lies among the sectors of sector group g, from g * 16 to (g + 1) * 16 - 1. source[j, g] differs from target[j, g] by at most 16. `live_count`: some device has all 48 slots live in every draw. `sector_sizes`: some sector has all 256 rows live in every draw.
All inputs are finite; a program needn't handle non-finite values.
Results may differ from the reference program's by a relative error of at most 0.0042.
Values may be sent and summed in bfloat16 or wider, within the bound.
A program may use at most 128 MiB of HBM per device.

```python
import jax
import jax.numpy as jnp
from jax import lax

M = 256
SEC_DEV = 16
SLOT_DEV = 48
SECTORS = 128
GROUPS = 8
TGROUPS = 4
SLOTS = 192


def pair_plan(key):
    base = jax.random.fold_in(key, 7)
    offset = jax.random.randint(jax.random.fold_in(base, 1), (SLOTS, GROUPS), 0, SEC_DEV)
    groups_iota = jnp.arange(GROUPS, dtype=jnp.int32)[None, :]
    target_ids = (groups_iota * SEC_DEV + offset).astype(jnp.int32)
    moved = jax.random.randint(jax.random.fold_in(base, 2), (SLOTS, GROUPS), -SEC_DEV, SEC_DEV + 1)
    source_ids = jnp.clip(target_ids + moved, 0, SECTORS - 1).astype(jnp.int32)
    return (target_ids, source_ids)


def draw_target(key, part):
    return pair_plan(key)[0]


def draw_source(key, part):
    return pair_plan(key)[1]


def draw_live_count(key, part):
    base = jax.random.fold_in(key, 11)
    counts = jax.random.randint(jax.random.fold_in(base, 1), (TGROUPS * GROUPS,), 1, SLOT_DEV + 1)
    spot = jax.random.randint(jax.random.fold_in(base, 2), (), 0, TGROUPS * GROUPS)
    counts = jnp.where(jnp.arange(TGROUPS * GROUPS) == spot, SLOT_DEV, counts)
    return counts.reshape(TGROUPS, GROUPS).astype(jnp.int32)


def draw_sector_sizes(key, part):
    base = jax.random.fold_in(key, 13)
    sizes_drawn = jax.random.randint(jax.random.fold_in(base, 1), (SECTORS,), M // 4, M + 1)
    spot = jax.random.randint(jax.random.fold_in(base, 2), (), 0, SECTORS)
    sizes_drawn = jnp.where(jnp.arange(SECTORS) == spot, M, sizes_drawn)
    return sizes_drawn.astype(jnp.int32)


def levels(own_key, dims, pieces, least, top_value):
    level = 1.0
    for dim, parts in pieces:
        draws = jax.random.uniform(jax.random.fold_in(jax.random.fold_in(own_key, 6), dim), (parts,), jnp.float32, least / len(pieces), top_value / len(pieces))
        level = level * jnp.repeat(jnp.exp(draws), dims[dim] // parts).reshape((-1,) + (1,) * (len(dims) - 1 - dim))
    return level


def normal_values(own_key, shape, spread, most, shards=(), held_as=jnp.bfloat16):
    values = spread * jax.random.normal(own_key, shape, jnp.float32)
    if shards:
        values = values * levels(own_key, shape, shards, -0.22, 0.18)
    return jnp.clip(values, -most, most).astype(held_as)


def setup_inputs(seed: int = 0) -> dict:
    arg_keys = jax.random.split(jax.random.key(seed), 8)
    return {
        "psi": normal_values(arg_keys[0], (SECTORS, M, M), 1.0, 6.0, ((0, 8),)),
        "sector_sizes": draw_sector_sizes(jax.random.fold_in(arg_keys[7], 71), 0),
        "left_env": normal_values(arg_keys[2], (SLOTS, GROUPS, M, M), (M * SLOTS // SEC_DEV) ** -0.5, 0.109375, ((0, 4), (1, 8))),
        "right_env": normal_values(arg_keys[3], (SLOTS, GROUPS, M, M), M ** -0.5, 0.375, ((0, 4), (1, 8))),
        "target": draw_target(jax.random.fold_in(arg_keys[7], 71), 0),
        "source": draw_source(jax.random.fold_in(arg_keys[7], 71), 0),
        "live_count": draw_live_count(jax.random.fold_in(arg_keys[7], 71), 0),
    }


def reference(psi, sector_sizes, left_env, right_env, target, source, live_count):
    index_row = jnp.arange(M, dtype=jnp.int32)
    keep = (index_row[None, :, None] < sector_sizes[:, None, None]) & (index_row[None, None, :] < sector_sizes[:, None, None])
    masked = jnp.where(keep, psi, jnp.zeros_like(psi))
    slot_ids = jnp.arange(SLOTS, dtype=jnp.int32)

    def visit(carry, inputs):
        left, right, tgt, src, slot = inputs
        picked = masked[src].astype(jnp.float32)
        inner = jnp.einsum("gab,gbc->gac", left.astype(jnp.float32), picked, precision=lax.Precision.HIGHEST).astype(jnp.bfloat16)
        contribution = jnp.einsum("gac,gdc->gad", inner.astype(jnp.float32), right.astype(jnp.float32), precision=lax.Precision.HIGHEST)
        alive = (slot % SLOT_DEV) < live_count[slot // SLOT_DEV]
        contribution = contribution * alive.astype(jnp.float32)[:, None, None]
        return carry.at[tgt].add(contribution), None

    start = jnp.zeros((SECTORS, M, M), jnp.float32)
    total, unused = lax.scan(visit, start, (left_env, right_env, target, source, slot_ids))
    return jnp.where(keep, total, jnp.zeros_like(total))
```

```python
import functools
import math

import jax
import jax.numpy as jnp
from jax import lax
from jax.experimental import pallas as pl
from jax.experimental.pallas import tpu as pltpu
from jax.sharding import PartitionSpec as P

MESH = pl.DeviceIdType.MESH
SIXTEENTHS = (8, 8)
PAIRS = (3, 2)
HOOKS = ((), ((0, 2), (1, 1)))
SPLITS = (2, 4)
UNROLL = 16


def pieces(count, parts):
    sizes = [count // parts + (i < count % parts) for i in range(parts)]
    return [(sum(sizes[:i]), sizes[i]) for i in range(parts)]


def layout(secs):
    stages, start = [], 0
    for share, parts in zip(SIXTEENTHS, SPLITS):
        count = secs * share // 16
        messages = [(start + at, n, i % 2) for i, (at, n) in enumerate(pieces(count, parts))]
        stages.append((start, count, messages))
        start += count
    return stages


def kernel(
    terms, groups,
    live_hbm, sizes_hbm, target_hbm, source_hbm, psi_ref, left_ref, right_ref,
    out_ref,
    pool, late, left, right, inner, running, kept, own, first_out, first_in, second_out, second_in,
    live_ref, sizes_ref, target_ref, source_ref, table, plan,
    load_sems, near_send, near_recv, far_send, far_recv, pass_send, pass_recv,
    first_send, first_recv, second_send, second_recv,
):
    secs, block = psi_ref.shape[0], psi_ref.shape[1]
    slots = left_ref.shape[0]
    rows = block // terms
    side = math.isqrt(terms)
    stages = layout(secs)
    early = stages[0][1]
    group, term = lax.axis_index("sector"), lax.axis_index("term")
    odd = lax.rem(group, 2)
    near = group + 1 - 2 * odd
    far = group - 1 + 2 * odd
    has_far = jnp.logical_and(far >= 0, far < groups)
    col, row = lax.rem(term, side), lax.div(term, side)
    odd_col, odd_row = lax.rem(col, 2), lax.rem(row, 2)
    col_mate = term + 1 - 2 * odd_col
    row_mate = term + (1 - 2 * odd_row) * side
    mate = odd * row_mate + (1 - odd) * col_mate
    mine = odd * odd_row + (1 - odd) * odd_col
    mine_there = odd * odd_col + (1 - odd) * odd_row

    def sector(rank):
        return odd * rank + (1 - odd) * (secs - 1 - rank)

    half = secs // 2
    ahead, behind = odd * half, (1 - odd) * half

    def psi_load(at, sem):
        return pltpu.make_async_copy(psi_ref.at[pl.ds(at, half)], pool.at[pl.ds(at, half)], load_sems.at[sem])

    sizes_load = pltpu.make_async_copy(sizes_hbm, sizes_ref, load_sems.at[2])
    live_load = pltpu.make_async_copy(live_hbm, live_ref, load_sems.at[3])
    target_load = pltpu.make_async_copy(target_hbm, target_ref, load_sems.at[4])
    source_load = pltpu.make_async_copy(source_hbm, source_ref, load_sems.at[5])
    left_load = pltpu.make_async_copy(left_ref, left, load_sems.at[6])
    right_load = pltpu.make_async_copy(right_ref, right, load_sems.at[7])
    sizes_load.start()
    psi_load(ahead, 0).start()
    psi_load(behind, 1).start()
    live_load.start()
    target_load.start()
    source_load.start()

    barrier = pltpu.get_barrier_semaphore()
    pl.semaphore_signal(barrier, inc=1, device_id={"sector": near}, device_id_type=MESH)
    for d in range(1, terms):
        pl.semaphore_signal(
            barrier, inc=1, device_id={"term": lax.rem(term + d, terms)}, device_id_type=MESH
        )

    @pl.when(has_far)
    def _():
        pl.semaphore_signal(barrier, inc=1, device_id={"sector": far}, device_id_type=MESH)

    index_row = lax.broadcasted_iota(jnp.int32, (block, block), 0)
    index_col = lax.broadcasted_iota(jnp.int32, (block, block), 1)
    reach = jnp.maximum(index_row, index_col)

    def mask(at):
        def one(i, carry):
            q = at + i
            pool[q] = jnp.where(reach < sizes_ref[q], pool[q], jnp.zeros((block, block), pool.dtype))
            return carry

        lax.fori_loop(0, half, one, 0, unroll=4)

    def landing(stage, rank):
        return pool.at[2 * secs + rank] if stage == 0 else late.at[rank - early]

    arrivals, pairs = [], []
    for stage, (start, count, messages) in enumerate(stages):
        paired = 2 * PAIRS[stage]
        for i in range(0, paired, 2):
            pairs.append((stage, start + i))
            arrivals.append((stage, start + i, True))
        arrivals.extend((stage, start + i, False) for i in range(paired, count))

    def far_copy(i, sending):
        stage, rank, paired = arrivals[i]
        if paired:
            rank = rank + (mine_there if sending else mine)
        return pltpu.make_async_remote_copy(
            pool.at[secs - 1 - sector(rank)], landing(stage, rank), far_send.at[i], far_recv.at[i],
            device_id={"sector": far}, device_id_type=MESH,
        )

    def pass_copy(i, sending):
        stage, rank = pairs[i]
        at = landing(stage, rank + (mine if sending else 1 - mine))
        return pltpu.make_async_remote_copy(
            at, at, pass_send.at[i], pass_recv.at[i], device_id={"term": mate}, device_id_type=MESH,
        )

    def arrival_of(pair):
        stage, rank = pairs[pair]
        return arrivals.index((stage, rank, True))

    near_copy = pltpu.make_async_remote_copy(
        pool.at[pl.ds(0, secs)], pool.at[pl.ds(secs, secs)], near_send, near_recv,
        device_id={"sector": near}, device_id_type=MESH,
    )

    sizes_load.wait()
    psi_load(ahead, 0).wait()
    left_load.start()
    mask(ahead)
    pl.semaphore_wait(barrier, terms + has_far.astype(jnp.int32))

    @pl.when(has_far)
    def _():
        for i, (stage, rank, paired) in enumerate(arrivals):
            if stage == 0:
                far_copy(i, True).start()

    psi_load(behind, 1).wait()
    right_load.start()
    mask(behind)

    @pl.when(has_far)
    def _():
        for i, (stage, rank, paired) in enumerate(arrivals):
            if stage > 0:
                far_copy(i, True).start()

    near_copy.start()

    live_load.wait()
    target_load.wait()
    source_load.wait()
    lane = lax.broadcasted_iota(jnp.int32, (slots, slots), 1)
    line = lax.broadcasted_iota(jnp.int32, (slots, slots), 0)
    slot = lax.broadcasted_iota(jnp.int32, (1, slots), 1)

    def as_column(values):
        return jnp.sum(jnp.where(lane == line, values, 0), axis=1, keepdims=True)

    tgt = jnp.where(slot < live_ref[0, 0], target_ref[...] - group * secs, secs)
    from_own = source_ref[...] - group * secs
    from_near = source_ref[...] - near * secs
    from_far = jnp.clip(source_ref[...] - far * secs, 0, secs - 1)
    far_rank = odd * from_far + (1 - odd) * (secs - 1 - from_far)
    is_own = (from_own >= 0) & (from_own < secs)
    is_near = (from_near >= 0) & (from_near < secs)
    key = tgt * slots + slot
    order = jnp.sum((key < as_column(key)).astype(jnp.int32), axis=1, keepdims=True)
    table[...] = jnp.zeros_like(table)
    for stage, (start, count, messages) in enumerate(stages):
        ready = jnp.where(far_rank < start + count, 2 * secs + far_rank, 0)
        src = jnp.where(is_own, from_own, jnp.where(is_near, secs + from_near, ready))
        code = as_column(slot + src * 256 + tgt * 65536)
        table[stage : stage + 1, 0:slots] = jnp.sum(jnp.where(order == lane, code, 0), axis=0, keepdims=True)
    sec = lax.broadcasted_iota(jnp.int32, (slots, 128), 1)
    ends = len(stages)
    table[ends : ends + 1, :] = jnp.sum((as_column(tgt) <= sec).astype(jnp.int32), axis=0, keepdims=True)
    plan_load = pltpu.make_async_copy(table, plan, load_sems.at[8])
    plan_load.start()
    plan_load.wait()

    def forward(pair):
        @pl.when(has_far)
        def _():
            far_copy(arrival_of(pair), False).wait_recv()
            pass_copy(pair, True).start()

    def hooks(stage, loop, step):
        for later in range(1, len(stages)):
            for i, hook in enumerate(HOOKS[later]):
                if later == stage + 1 and hook is not None and hook[0] == loop:
                    pair = sum(PAIRS[:later]) + i

                    @pl.when(step == hook[1])
                    def _():
                        forward(pair)

    def receive(stage):
        start, count, messages = stages[stage]
        for i in range(PAIRS[stage]):
            if stage == 0 or HOOKS[stage][i] is None:
                forward(sum(PAIRS[:stage]) + i)

        @pl.when(has_far)
        def _():
            for i, (at, rank, paired) in enumerate(arrivals):
                if at == stage and not paired:
                    far_copy(i, False).wait_recv()
            for i, (at, rank) in enumerate(pairs):
                if at == stage:
                    pass_copy(i, False).wait_recv()
            if stage > 0:
                for i in range(count):
                    pool[2 * secs + start + i] = late[start + i - early]

    def compute(stage):
        def multiply(step, carry):
            hooks(stage, 0, step)
            for u in range(UNROLL):
                k = step * UNROLL + u
                code = plan[stage, k]
                inner[k] = jnp.dot(
                    left[code & 255], pool[(code >> 8) & 255], preferred_element_type=jnp.float32
                ).astype(jnp.bfloat16)
            return carry

        lax.fori_loop(0, slots // UNROLL, multiply, 0)

        def visit(step, carry):
            hooks(stage, 1, step)
            total = running[jnp.maximum(step * UNROLL - 1, 0)]
            for u in range(UNROLL):
                k = step * UNROLL + u
                code = plan[stage, k]
                again = jnp.logical_and(k > 0, (plan[stage, jnp.maximum(k - 1, 0)] >> 16) == (code >> 16))
                here = lax.dot_general(
                    inner[k], right[code & 255], (((1,), (1,)), ((), ())), preferred_element_type=jnp.float32
                )
                total = here + jnp.where(again, total, jnp.zeros_like(total))
                running[k] = total
            return carry

        lax.fori_loop(0, slots // UNROLL, visit, 0)

    def places(way):
        return (row, col) if way else (col, row)

    def term_at(way, first, second):
        return first * side + second if way else second * side + first

    numbers = {}
    for stage, (start, count, messages) in enumerate(stages):
        for message in messages:
            numbers[message] = len(numbers)

    def first_copy(message, d):
        at, n, way = message
        first, second = places(way)
        ranks, number = pl.ds(at, n), numbers[message]
        return pltpu.make_async_remote_copy(
            first_out.at[d - 1, ranks], first_in.at[d - 1, ranks],
            first_send.at[number, d - 1], first_recv.at[number, d - 1],
            device_id={"term": term_at(way, lax.rem(first + d, side), second)}, device_id_type=MESH,
        )

    def second_copy(message, d):
        at, n, way = message
        first, second = places(way)
        ranks, number = pl.ds(at, n), numbers[message]
        return pltpu.make_async_remote_copy(
            second_out.at[d - 1, ranks], second_in.at[d - 1, ranks],
            second_send.at[number, d - 1], second_recv.at[number, d - 1],
            device_id={"term": term_at(way, first, lax.rem(second + d, side))}, device_id_type=MESH,
        )

    def give(message):
        at, n, way = message
        first, second = places(way)
        for rank in range(at, at + n):
            q = sector(rank)
            end = plan[ends, q]
            start = jnp.where(q > 0, plan[ends, jnp.maximum(q - 1, 0)], 0)
            for d in range(side):
                for b in range(side):
                    line = pl.multiple_of(term_at(way, lax.rem(first + d, side), b) * rows, rows)
                    total = running[jnp.maximum(end - 1, 0), pl.ds(line, rows), :]
                    total = jnp.where(end > start, total, jnp.zeros_like(total))
                    if d:
                        first_out[d - 1, rank, b] = total.astype(first_out.dtype)
                    else:
                        kept[rank, b] = total
        for d in range(1, side):
            first_copy(message, d).start()

    def pass_on(message):
        at, n, way = message
        first, second = places(way)
        for d in range(1, side):
            first_copy(message, d).wait_recv()
        for rank in range(at, at + n):
            for e in range(side):
                b = lax.rem(second + e, side)
                total = kept[rank, b]
                for d in range(1, side):
                    total = total + first_in[d - 1, rank, b].astype(jnp.float32)
                if e:
                    second_out[e - 1, rank] = total.astype(second_out.dtype)
                else:
                    own[rank] = total
        for e in range(1, side):
            second_copy(message, e).start()

    kept_row = lax.broadcasted_iota(jnp.int32, (rows, block), 0) + term * rows
    kept_col = lax.broadcasted_iota(jnp.int32, (rows, block), 1)
    kept_reach = jnp.maximum(kept_row, kept_col)

    def finish(message):
        at, n, way = message
        for d in range(1, side):
            second_copy(message, d).wait_recv()
        for rank in range(at, at + n):
            q = sector(rank)
            total = own[rank]
            for d in range(1, side):
                total = total + second_in[d - 1, rank].astype(jnp.float32)
            out_ref[q] = jnp.where(kept_reach < sizes_ref[q], total, jnp.zeros_like(total))

    for stage, (start, count, messages) in enumerate(stages):
        receive(stage)
        if stage == 0:
            near_copy.wait_recv()
            left_load.wait()
            right_load.wait()
        compute(stage)
        for message in messages:
            give(message)
        if stage > 0:
            for message in stages[stage - 1][2]:
                pass_on(message)
    for message in stages[-1][2]:
        pass_on(message)
    for stage, (start, count, messages) in enumerate(stages):
        for message in messages:
            finish(message)

    near_copy.wait_send()

    @pl.when(has_far)
    def _():
        for i in range(len(arrivals)):
            far_copy(i, True).wait_send()
        for i in range(len(pairs)):
            pass_copy(i, True).wait_send()

    for message in numbers:
        for d in range(1, side):
            first_copy(message, d).wait_send()
            second_copy(message, d).wait_send()


def on_device(terms, groups, psi, sector_sizes, left_env, right_env, target, source, live_count):
    secs, block = psi.shape[0], psi.shape[1]
    slots = left_env.shape[0]
    rows, side = block // terms, math.isqrt(terms)
    stages = layout(secs)
    late = secs - stages[0][1]
    messages = sum(len(stage[2]) for stage in stages)
    coming = secs - sum(PAIRS)
    dma = pltpu.SemaphoreType.DMA
    here, vmem = pl.BlockSpec(memory_space=pl.ANY), pl.BlockSpec(memory_space=pltpu.VMEM)
    return pl.pallas_call(
        functools.partial(kernel, terms, groups),
        out_shape=jax.ShapeDtypeStruct((secs, rows, block), jnp.float32),
        in_specs=[here] * 7,
        out_specs=vmem,
        scratch_shapes=[
            pltpu.VMEM((3 * secs, block, block), jnp.bfloat16),
            pltpu.VMEM((late, block, block), jnp.bfloat16),
            pltpu.VMEM((slots, block, block), jnp.bfloat16),
            pltpu.VMEM((slots, block, block), jnp.bfloat16),
            pltpu.VMEM((slots, block, block), jnp.bfloat16),
            pltpu.VMEM((slots, block, block), jnp.float32),
            pltpu.VMEM((secs, side, rows, block), jnp.float32),
            pltpu.VMEM((secs, rows, block), jnp.float32),
            pltpu.VMEM((side - 1, secs, side, rows, block), jnp.bfloat16),
            pltpu.VMEM((side - 1, secs, side, rows, block), jnp.bfloat16),
            pltpu.VMEM((side - 1, secs, rows, block), jnp.bfloat16),
            pltpu.VMEM((side - 1, secs, rows, block), jnp.bfloat16),
            pltpu.SMEM((1, 1), jnp.int32),
            pltpu.SMEM((secs,), jnp.int32),
            pltpu.VMEM((1, slots), jnp.int32),
            pltpu.VMEM((1, slots), jnp.int32),
            pltpu.VMEM((8, 128), jnp.int32),
            pltpu.SMEM((8, 128), jnp.int32),
            dma((9,)), dma, dma, dma((coming,)), dma((coming,)), dma((sum(PAIRS),)), dma((sum(PAIRS),)),
            *[dma((messages, side - 1))] * 4,
        ],
        compiler_params=pltpu.CompilerParams(
            collective_id=0, has_side_effects=True, vmem_limit_bytes=52 * 1024 * 1024
        ),
    )(
        live_count, sector_sizes, target.reshape(1, slots), source.reshape(1, slots),
        psi, left_env[:, 0], right_env[:, 0],
    )


def solution(mesh):
    placed = (
        P("sector", None, None),
        P("sector"),
        P("term", "sector", None, None),
        P("term", "sector", None, None),
        P("term", "sector"),
        P("term", "sector"),
        P("term", "sector"),
    )
    return jax.shard_map(
        functools.partial(on_device, mesh.shape["term"], mesh.shape["sector"]),
        mesh=mesh, in_specs=placed, out_specs=P("sector", "term", None), check_vma=False,
    )
```

```python
import functools
import math

import jax
import jax.numpy as jnp
from jax import lax
from jax.experimental import pallas as pl
from jax.experimental.pallas import tpu as pltpu
from jax.sharding import PartitionSpec as P

MESH = pl.DeviceIdType.MESH
SIXTEENTHS = (8, 8)
PAIRS = (3, 2)
HOOKS = ((), ((0, 16), (1, 0)))
SUMS = ((), ((1, 0), (1, 0), None, None))
SPLITS = (4, 4)


def pieces(count, parts):
    sizes = [count // parts + (i < count % parts) for i in range(parts)]
    return [(sum(sizes[:i]), sizes[i]) for i in range(parts)]


def layout(secs):
    stages, start = [], 0
    for share, parts in zip(SIXTEENTHS, SPLITS):
        count = secs * share // 16
        messages = [(start + at, n, i % 2) for i, (at, n) in enumerate(pieces(count, parts))]
        stages.append((start, count, messages))
        start += count
    return stages


def kernel(
    terms, groups,
    packed_ref, psi_ref, left_ref, right_ref,
    out_ref,
    pool, late, left, right, inner, running, kept, own, first_out, first_in, second_out, second_in,
    packed_scalars, table, plan,
    load_sems, near_send, near_recv, far_send, far_recv, pass_send, pass_recv,
    first_send, first_recv, second_send, second_recv,
):
    secs, block = psi_ref.shape[0], psi_ref.shape[1]
    slots = left_ref.shape[0]
    rows = block // terms
    side = math.isqrt(terms)
    stages = layout(secs)
    early = stages[0][1]
    group, term = lax.axis_index("sector"), lax.axis_index("term")
    odd = lax.rem(group, 2)
    near = group + 1 - 2 * odd
    far = group - 1 + 2 * odd
    has_far = jnp.logical_and(far >= 0, far < groups)
    col, row = lax.rem(term, side), lax.div(term, side)
    odd_col, odd_row = lax.rem(col, 2), lax.rem(row, 2)
    col_mate = term + 1 - 2 * odd_col
    row_mate = term + (1 - 2 * odd_row) * side
    mate = odd * row_mate + (1 - odd) * col_mate
    mine = odd * odd_row + (1 - odd) * odd_col
    mine_there = odd * odd_col + (1 - odd) * odd_row

    def sector(rank):
        return odd * rank + (1 - odd) * (secs - 1 - rank)

    half = secs // 2
    ahead, behind = odd * half, (1 - odd) * half

    def psi_load(at, sem):
        return pltpu.make_async_copy(psi_ref.at[pl.ds(at, half)], pool.at[pl.ds(at, half)], load_sems.at[sem])

    sizes_load = pltpu.make_async_copy(packed_ref, packed_scalars, load_sems.at[2])
    left_load = pltpu.make_async_copy(left_ref, left, load_sems.at[6])
    right_load = pltpu.make_async_copy(right_ref, right, load_sems.at[7])
    sizes_load.start()
    psi_load(ahead, 0).start()
    psi_load(behind, 1).start()

    barrier = pltpu.get_barrier_semaphore()
    pl.semaphore_signal(barrier, inc=1, device_id={"sector": near}, device_id_type=MESH)
    for d in range(1, terms):
        pl.semaphore_signal(
            barrier, inc=1, device_id={"term": lax.rem(term + d, terms)}, device_id_type=MESH
        )

    @pl.when(has_far)
    def _():
        pl.semaphore_signal(barrier, inc=1, device_id={"sector": far}, device_id_type=MESH)

    index_row = lax.broadcasted_iota(jnp.int32, (block, block), 0)
    index_col = lax.broadcasted_iota(jnp.int32, (block, block), 1)
    reach = jnp.maximum(index_row, index_col)

    def mask(at):
        def one(i, carry):
            q = at + i
            pool[q] = jnp.where(reach < packed_scalars[0, 2 * slots + q], pool[q], jnp.zeros((block, block), pool.dtype))
            return carry

        lax.fori_loop(0, half, one, 0, unroll=4)

    def landing(stage, rank):
        return pool.at[2 * secs + rank] if stage == 0 else late.at[rank - early]

    arrivals, pairs = [], []
    for stage, (start, count, messages) in enumerate(stages):
        paired = 2 * PAIRS[stage]
        for i in range(0, paired, 2):
            pairs.append((stage, start + i))
            arrivals.append((stage, start + i, True))
        arrivals.extend((stage, start + i, False) for i in range(paired, count))

    def far_copy(i, sending):
        stage, rank, paired = arrivals[i]
        if paired:
            rank = rank + (mine_there if sending else mine)
        return pltpu.make_async_remote_copy(
            pool.at[secs - 1 - sector(rank)], landing(stage, rank), far_send.at[i], far_recv.at[i],
            device_id={"sector": far}, device_id_type=MESH,
        )

    def pass_copy(i, sending):
        stage, rank = pairs[i]
        at = landing(stage, rank + (mine if sending else 1 - mine))
        return pltpu.make_async_remote_copy(
            at, at, pass_send.at[i], pass_recv.at[i], device_id={"term": mate}, device_id_type=MESH,
        )

    def arrival_of(pair):
        stage, rank = pairs[pair]
        return arrivals.index((stage, rank, True))

    near_copy = pltpu.make_async_remote_copy(
        pool.at[pl.ds(0, secs)], pool.at[pl.ds(secs, secs)], near_send, near_recv,
        device_id={"sector": near}, device_id_type=MESH,
    )

    sizes_load.wait()
    psi_load(ahead, 0).wait()
    left_load.start()
    mask(ahead)
    pl.semaphore_wait(barrier, terms + has_far.astype(jnp.int32))

    @pl.when(has_far)
    def _():
        for i, (stage, rank, paired) in enumerate(arrivals):
            if stage == 0:
                far_copy(i, True).start()

    psi_load(behind, 1).wait()
    right_load.start()
    mask(behind)

    @pl.when(has_far)
    def _():
        for i, (stage, rank, paired) in enumerate(arrivals):
            if stage > 0:
                far_copy(i, True).start()

    near_copy.start()

    lane = lax.broadcasted_iota(jnp.int32, (slots, slots), 1)
    line = lax.broadcasted_iota(jnp.int32, (slots, slots), 0)
    slot = lax.broadcasted_iota(jnp.int32, (1, slots), 1)

    def as_column(values):
        return jnp.sum(jnp.where(lane == line, values, 0), axis=1, keepdims=True)

    tgt = jnp.where(slot < packed_scalars[0, 2 * slots + secs], packed_ref[:, 0:slots] - group * secs, secs)
    from_own = packed_ref[:, slots : 2 * slots] - group * secs
    from_near = packed_ref[:, slots : 2 * slots] - near * secs
    from_far = jnp.clip(packed_ref[:, slots : 2 * slots] - far * secs, 0, secs - 1)
    far_rank = odd * from_far + (1 - odd) * (secs - 1 - from_far)
    is_own = (from_own >= 0) & (from_own < secs)
    is_near = (from_near >= 0) & (from_near < secs)
    key = tgt * slots + slot
    order = jnp.sum((key < as_column(key)).astype(jnp.int32), axis=1, keepdims=True)
    table[...] = jnp.zeros_like(table)
    for stage, (start, count, messages) in enumerate(stages):
        ready = jnp.where(far_rank < start + count, 2 * secs + far_rank, 0)
        src = jnp.where(is_own, from_own, jnp.where(is_near, secs + from_near, ready))
        code = as_column(slot + src * 256 + tgt * 65536)
        table[stage : stage + 1, 0:slots] = jnp.sum(jnp.where(order == lane, code, 0), axis=0, keepdims=True)
    sec = lax.broadcasted_iota(jnp.int32, (slots, 128), 1)
    ends = len(stages)
    table[ends : ends + 1, :] = jnp.sum((as_column(tgt) <= sec).astype(jnp.int32), axis=0, keepdims=True)
    plan_load = pltpu.make_async_copy(table, plan, load_sems.at[8])
    plan_load.start()
    plan_load.wait()

    def forward(pair):
        @pl.when(has_far)
        def _():
            far_copy(arrival_of(pair), False).wait_recv()
            pass_copy(pair, True).start()

    def hooks(stage, loop, k):
        if stage + 1 < len(stages):
            for i, hook in enumerate(HOOKS[stage + 1]):
                if hook == (loop, k):
                    forward(sum(PAIRS[: stage + 1]) + i)
        if stage > 0:
            for i, hook in enumerate(SUMS[stage]):
                if hook == (loop, k):
                    pass_on(stages[stage - 1][2][i])

    def receive(stage):
        start, count, messages = stages[stage]
        for i in range(PAIRS[stage]):
            if stage == 0 or HOOKS[stage][i] is None:
                forward(sum(PAIRS[:stage]) + i)

        @pl.when(has_far)
        def _():
            for i, (at, rank, paired) in enumerate(arrivals):
                if at == stage and not paired:
                    far_copy(i, False).wait_recv()
            for i, (at, rank) in enumerate(pairs):
                if at == stage:
                    pass_copy(i, False).wait_recv()
            if stage > 0:
                for i in range(count):
                    pool[2 * secs + start + i] = late[start + i - early]

    def compute(stage):
        for k in range(slots):
            hooks(stage, 0, k)
            code = plan[stage, k]
            inner[k] = jnp.dot(
                left[code & 255], pool[(code >> 8) & 255], preferred_element_type=jnp.float32
            ).astype(jnp.bfloat16)
        total, before = jnp.zeros((block, block), jnp.float32), secs
        for k in range(slots):
            hooks(stage, 1, k)
            code = plan[stage, k]
            tgt = code >> 16
            here = lax.dot_general(
                inner[k], right[code & 255], (((1,), (1,)), ((), ())), preferred_element_type=jnp.float32
            )
            total = here + jnp.where(tgt == before, total, jnp.zeros_like(total)) if k else here
            running[k] = total
            before = tgt
        hooks(stage, 2, 0)

    def places(way):
        return (row, col) if way else (col, row)

    def term_at(way, first, second):
        return first * side + second if way else second * side + first

    numbers = {}
    for stage, (start, count, messages) in enumerate(stages):
        for message in messages:
            numbers[message] = len(numbers)

    def first_copy(message, d):
        at, n, way = message
        first, second = places(way)
        ranks, number = pl.ds(at, n), numbers[message]
        return pltpu.make_async_remote_copy(
            first_out.at[d - 1, ranks], first_in.at[d - 1, ranks],
            first_send.at[number, d - 1], first_recv.at[number, d - 1],
            device_id={"term": term_at(way, lax.rem(first + d, side), second)}, device_id_type=MESH,
        )

    def second_copy(message, d):
        at, n, way = message
        first, second = places(way)
        ranks, number = pl.ds(at, n), numbers[message]
        return pltpu.make_async_remote_copy(
            second_out.at[d - 1, ranks], second_in.at[d - 1, ranks],
            second_send.at[number, d - 1], second_recv.at[number, d - 1],
            device_id={"term": term_at(way, first, lax.rem(second + d, side))}, device_id_type=MESH,
        )

    def give(message):
        at, n, way = message
        first, second = places(way)
        for rank in range(at, at + n):
            q = sector(rank)
            end = plan[ends, q]
            start = jnp.where(q > 0, plan[ends, jnp.maximum(q - 1, 0)], 0)
            for d in range(side):
                for b in range(side):
                    line = pl.multiple_of(term_at(way, lax.rem(first + d, side), b) * rows, rows)
                    total = running[jnp.maximum(end - 1, 0), pl.ds(line, rows), :]
                    total = jnp.where(end > start, total, jnp.zeros_like(total))
                    if d:
                        first_out[d - 1, rank, b] = total.astype(first_out.dtype)
                    else:
                        kept[rank, b] = total
        for d in range(1, side):
            first_copy(message, d).start()

    def pass_on(message):
        at, n, way = message
        first, second = places(way)
        for d in range(1, side):
            first_copy(message, d).wait_recv()
        for rank in range(at, at + n):
            for e in range(side):
                b = lax.rem(second + e, side)
                total = kept[rank, b]
                for d in range(1, side):
                    total = total + first_in[d - 1, rank, b].astype(jnp.float32)
                if e:
                    second_out[e - 1, rank] = total.astype(second_out.dtype)
                else:
                    own[rank] = total
        for e in range(1, side):
            second_copy(message, e).start()

    kept_row = lax.broadcasted_iota(jnp.int32, (rows, block), 0) + term * rows
    kept_col = lax.broadcasted_iota(jnp.int32, (rows, block), 1)
    kept_reach = jnp.maximum(kept_row, kept_col)

    def finish(message):
        at, n, way = message
        for d in range(1, side):
            second_copy(message, d).wait_recv()
        for rank in range(at, at + n):
            q = sector(rank)
            total = own[rank]
            for d in range(1, side):
                total = total + second_in[d - 1, rank].astype(jnp.float32)
            out_ref[q] = jnp.where(kept_reach < packed_scalars[0, 2 * slots + q], total, jnp.zeros_like(total))

    for stage, (start, count, messages) in enumerate(stages):
        receive(stage)
        if stage == 0:
            near_copy.wait_recv()
            left_load.wait()
            right_load.wait()
        compute(stage)
        for message in messages:
            give(message)
        if stage > 0:
            for i, message in enumerate(stages[stage - 1][2]):
                if SUMS[stage][i] is None:
                    pass_on(message)
    for message in stages[-1][2]:
        pass_on(message)
    for stage, (start, count, messages) in enumerate(stages):
        for message in messages:
            finish(message)

    near_copy.wait_send()

    @pl.when(has_far)
    def _():
        for i in range(len(arrivals)):
            far_copy(i, True).wait_send()
        for i in range(len(pairs)):
            pass_copy(i, True).wait_send()

    for message in numbers:
        for d in range(1, side):
            first_copy(message, d).wait_send()
            second_copy(message, d).wait_send()


def on_device(terms, groups, psi, sector_sizes, left_env, right_env, target, source, live_count):
    secs, block = psi.shape[0], psi.shape[1]
    slots = left_env.shape[0]
    rows, side = block // terms, math.isqrt(terms)
    stages = layout(secs)
    late = secs - stages[0][1]
    messages = sum(len(stage[2]) for stage in stages)
    coming = secs - sum(PAIRS)
    dma = pltpu.SemaphoreType.DMA
    here, vmem = pl.BlockSpec(memory_space=pl.ANY), pl.BlockSpec(memory_space=pltpu.VMEM)
    packed = jnp.concatenate(
        [target.reshape(1, slots), source.reshape(1, slots), sector_sizes.reshape(1, secs), live_count], axis=1
    )
    return pl.pallas_call(
        functools.partial(kernel, terms, groups),
        out_shape=jax.ShapeDtypeStruct((secs, rows, block), jnp.float32),
        in_specs=[vmem] + [here] * 3,
        out_specs=vmem,
        scratch_shapes=[
            pltpu.VMEM((3 * secs, block, block), jnp.bfloat16),
            pltpu.VMEM((late, block, block), jnp.bfloat16),
            pltpu.VMEM((slots, block, block), jnp.bfloat16),
            pltpu.VMEM((slots, block, block), jnp.bfloat16),
            pltpu.VMEM((slots, block, block), jnp.bfloat16),
            pltpu.VMEM((slots, block, block), jnp.float32),
            pltpu.VMEM((secs, side, rows, block), jnp.float32),
            pltpu.VMEM((secs, rows, block), jnp.float32),
            pltpu.VMEM((side - 1, secs, side, rows, block), jnp.bfloat16),
            pltpu.VMEM((side - 1, secs, side, rows, block), jnp.bfloat16),
            pltpu.VMEM((side - 1, secs, rows, block), jnp.bfloat16),
            pltpu.VMEM((side - 1, secs, rows, block), jnp.bfloat16),
            pltpu.SMEM((1, 2 * slots + secs + 1), jnp.int32),
            pltpu.VMEM((8, 128), jnp.int32),
            pltpu.SMEM((8, 128), jnp.int32),
            dma((9,)), dma, dma, dma((coming,)), dma((coming,)), dma((sum(PAIRS),)), dma((sum(PAIRS),)),
            *[dma((messages, side - 1))] * 4,
        ],
        compiler_params=pltpu.CompilerParams(
            collective_id=0, has_side_effects=True, vmem_limit_bytes=52 * 1024 * 1024
        ),
    )(
        packed,
        psi, left_env[:, 0], right_env[:, 0],
    )


def solution(mesh):
    placed = (
        P("sector", None, None),
        P("sector"),
        P("term", "sector", None, None),
        P("term", "sector", None, None),
        P("term", "sector"),
        P("term", "sector"),
        P("term", "sector"),
    )
    return jax.shard_map(
        functools.partial(on_device, mesh.shape["term"], mesh.shape["sector"]),
        mesh=mesh, in_specs=placed, out_specs=P("sector", "term", None), check_vma=False,
    )
```

```python
import functools
import math

import jax
import jax.numpy as jnp
from jax import lax
from jax.experimental import pallas as pl
from jax.experimental.pallas import tpu as pltpu
from jax.sharding import PartitionSpec as P

MESH = pl.DeviceIdType.MESH
SIXTEENTHS = (8, 8)
PARTS = 2
PAIRS = (3, 2)
HOOKS = ((), ((0, 16), (1, 0)))
SUMS = ((), ((1, 0), (1, 0), None, None))
SPLITS = (4, 4)


def pieces(count, parts):
    sizes = [count // parts + (i < count % parts) for i in range(parts)]
    return [(sum(sizes[:i]), sizes[i]) for i in range(parts)]


def layout(secs):
    stages, start = [], 0
    for share, parts in zip(SIXTEENTHS, SPLITS):
        count = secs * share // 16
        messages = [(start + at, n, i % 2) for i, (at, n) in enumerate(pieces(count, parts))]
        stages.append((start, count, messages))
        start += count
    return stages


def kernel(
    terms, groups,
    packed_ref, psi_ref, left_ref, right_ref,
    out_ref,
    pool, late, left, right, inner, running, kept, own, first_out, first_in, second_out, second_in,
    packed_scalars, table, plan,
    load_sems, near_send, near_recv, far_send, far_recv, pass_send, pass_recv,
    first_send, first_recv, second_send, second_recv,
):
    secs, block = psi_ref.shape[0], psi_ref.shape[1]
    slots = left_ref.shape[0]
    rows = block // terms
    side = math.isqrt(terms)
    stages = layout(secs)
    early = stages[0][1]
    group, term = lax.axis_index("sector"), lax.axis_index("term")
    odd = lax.rem(group, 2)
    near = group + 1 - 2 * odd
    far = group - 1 + 2 * odd
    has_far = jnp.logical_and(far >= 0, far < groups)
    col, row = lax.rem(term, side), lax.div(term, side)
    odd_col, odd_row = lax.rem(col, 2), lax.rem(row, 2)
    col_mate = term + 1 - 2 * odd_col
    row_mate = term + (1 - 2 * odd_row) * side
    mate = odd * row_mate + (1 - odd) * col_mate
    mine = odd * odd_row + (1 - odd) * odd_col
    mine_there = odd * odd_col + (1 - odd) * odd_row

    def sector(rank):
        return odd * rank + (1 - odd) * (secs - 1 - rank)

    half = secs // 2
    ahead, behind = odd * half, (1 - odd) * half

    def psi_load(at, sem):
        return pltpu.make_async_copy(psi_ref.at[pl.ds(at, half)], pool.at[pl.ds(at, half)], load_sems.at[sem])

    sizes_load = pltpu.make_async_copy(packed_ref, packed_scalars, load_sems.at[2])
    left_load = pltpu.make_async_copy(left_ref, left, load_sems.at[6])
    right_load = pltpu.make_async_copy(right_ref, right, load_sems.at[7])
    sizes_load.start()
    psi_load(ahead, 0).start()
    psi_load(behind, 1).start()

    barrier = pltpu.get_barrier_semaphore()
    pl.semaphore_signal(barrier, inc=1, device_id={"sector": near}, device_id_type=MESH)
    for d in range(1, side):
        for other in (row * side + lax.rem(col + d, side), lax.rem(row + d, side) * side + col):
            pl.semaphore_signal(barrier, inc=1, device_id={"term": other}, device_id_type=MESH)

    @pl.when(has_far)
    def _():
        pl.semaphore_signal(barrier, inc=1, device_id={"sector": far}, device_id_type=MESH)

    index_row = lax.broadcasted_iota(jnp.int32, (block, block), 0)
    index_col = lax.broadcasted_iota(jnp.int32, (block, block), 1)
    reach = jnp.maximum(index_row, index_col)

    def mask(at):
        def one(i, carry):
            q = at + i
            pool[q] = jnp.where(reach < packed_scalars[0, 2 * slots + q], pool[q], jnp.zeros((block, block), pool.dtype))
            return carry

        lax.fori_loop(0, half, one, 0, unroll=4)

    def landing(stage, rank):
        return pool.at[2 * secs + rank] if stage == 0 else late.at[rank - early]

    arrivals, pairs = [], []
    for stage, (start, count, messages) in enumerate(stages):
        paired = 2 * PAIRS[stage]
        for i in range(0, paired, 2):
            for part in range(PARTS):
                pairs.append((stage, start + i, part))
                arrivals.append((stage, start + i, part))
        arrivals.extend((stage, start + i, None) for i in range(paired, count))
    size = block // PARTS

    def part_of(ref, part):
        return ref if part is None else ref.at[pl.ds(part * size, size)]

    def far_copy(i, sending):
        stage, rank, part = arrivals[i]
        if part is not None:
            rank = rank + (mine_there if sending else mine)
        return pltpu.make_async_remote_copy(
            part_of(pool.at[secs - 1 - sector(rank)], part), part_of(landing(stage, rank), part),
            far_send.at[i], far_recv.at[i],
            device_id={"sector": far}, device_id_type=MESH,
        )

    def pass_copy(i, sending):
        stage, rank, part = pairs[i]
        at = part_of(landing(stage, rank + (mine if sending else 1 - mine)), part)
        return pltpu.make_async_remote_copy(
            at, at, pass_send.at[i], pass_recv.at[i], device_id={"term": mate}, device_id_type=MESH,
        )

    def arrival_of(pair):
        return arrivals.index(pairs[pair])

    near_copy = pltpu.make_async_remote_copy(
        pool.at[pl.ds(0, secs)], pool.at[pl.ds(secs, secs)], near_send, near_recv,
        device_id={"sector": near}, device_id_type=MESH,
    )

    sizes_load.wait()
    psi_load(ahead, 0).wait()
    left_load.start()
    mask(ahead)
    pl.semaphore_wait(barrier, 2 * side - 1 + has_far.astype(jnp.int32))

    @pl.when(has_far)
    def _():
        for i, (stage, rank, part) in enumerate(arrivals):
            if stage == 0:
                far_copy(i, True).start()

    psi_load(behind, 1).wait()
    right_load.start()
    mask(behind)

    @pl.when(has_far)
    def _():
        for i, (stage, rank, part) in enumerate(arrivals):
            if stage > 0:
                far_copy(i, True).start()

    near_copy.start()

    lane = lax.broadcasted_iota(jnp.int32, (slots, slots), 1)
    line = lax.broadcasted_iota(jnp.int32, (slots, slots), 0)
    slot = lax.broadcasted_iota(jnp.int32, (1, slots), 1)

    def as_column(values):
        return jnp.sum(jnp.where(lane == line, values, 0), axis=1, keepdims=True)

    tgt = jnp.where(slot < packed_scalars[0, 2 * slots + secs], packed_ref[:, 0:slots] - group * secs, secs)
    from_own = packed_ref[:, slots : 2 * slots] - group * secs
    from_near = packed_ref[:, slots : 2 * slots] - near * secs
    from_far = jnp.clip(packed_ref[:, slots : 2 * slots] - far * secs, 0, secs - 1)
    far_rank = odd * from_far + (1 - odd) * (secs - 1 - from_far)
    is_own = (from_own >= 0) & (from_own < secs)
    is_near = (from_near >= 0) & (from_near < secs)
    key = tgt * slots + slot
    order = jnp.sum((key < as_column(key)).astype(jnp.int32), axis=1, keepdims=True)
    table[...] = jnp.zeros_like(table)
    for stage, (start, count, messages) in enumerate(stages):
        ready = jnp.where(far_rank < start + count, 2 * secs + far_rank, 0)
        src = jnp.where(is_own, from_own, jnp.where(is_near, secs + from_near, ready))
        code = as_column(slot + src * 256 + tgt * 65536)
        table[stage : stage + 1, 0:slots] = jnp.sum(jnp.where(order == lane, code, 0), axis=0, keepdims=True)
    sec = lax.broadcasted_iota(jnp.int32, (slots, 128), 1)
    ends = len(stages)
    table[ends : ends + 1, :] = jnp.sum((as_column(tgt) <= sec).astype(jnp.int32), axis=0, keepdims=True)
    plan_load = pltpu.make_async_copy(table, plan, load_sems.at[8])
    plan_load.start()
    plan_load.wait()

    def forward(pair):
        @pl.when(has_far)
        def _():
            for i in range(PARTS * pair, PARTS * (pair + 1)):
                far_copy(arrival_of(i), False).wait_recv()
                pass_copy(i, True).start()

    def hooks(stage, loop, k):
        if stage + 1 < len(stages):
            for i, hook in enumerate(HOOKS[stage + 1]):
                if hook == (loop, k):
                    forward(sum(PAIRS[: stage + 1]) + i)
        if stage > 0:
            for i, hook in enumerate(SUMS[stage]):
                if hook == (loop, k):
                    pass_on(stages[stage - 1][2][i])

    def receive(stage):
        start, count, messages = stages[stage]
        for i in range(PAIRS[stage]):
            if stage == 0 or HOOKS[stage][i] is None:
                forward(sum(PAIRS[:stage]) + i)

        @pl.when(has_far)
        def _():
            for i, (at, rank, part) in enumerate(arrivals):
                if at == stage and part is None:
                    far_copy(i, False).wait_recv()
            for i, (at, rank, part) in enumerate(pairs):
                if at == stage:
                    pass_copy(i, False).wait_recv()
            if stage > 0:
                for i in range(count):
                    pool[2 * secs + start + i] = late[start + i - early]

    def compute(stage):
        for k in range(slots):
            hooks(stage, 0, k)
            code = plan[stage, k]
            inner[k] = jnp.dot(
                left[code & 255], pool[(code >> 8) & 255], preferred_element_type=jnp.float32
            ).astype(jnp.bfloat16)
        total, before = jnp.zeros((block, block), jnp.float32), secs
        for k in range(slots):
            hooks(stage, 1, k)
            code = plan[stage, k]
            tgt = code >> 16
            here = lax.dot_general(
                inner[k], right[code & 255], (((1,), (1,)), ((), ())), preferred_element_type=jnp.float32
            )
            total = here + jnp.where(tgt == before, total, jnp.zeros_like(total)) if k else here
            running[k] = total
            before = tgt
        hooks(stage, 2, 0)

    def places(way):
        return (row, col) if way else (col, row)

    def term_at(way, first, second):
        return first * side + second if way else second * side + first

    numbers = {}
    for stage, (start, count, messages) in enumerate(stages):
        for message in messages:
            numbers[message] = len(numbers)

    def first_copy(message, d):
        at, n, way = message
        first, second = places(way)
        ranks, number = pl.ds(at, n), numbers[message]
        return pltpu.make_async_remote_copy(
            first_out.at[d - 1, ranks], first_in.at[d - 1, ranks],
            first_send.at[number, d - 1], first_recv.at[number, d - 1],
            device_id={"term": term_at(way, lax.rem(first + d, side), second)}, device_id_type=MESH,
        )

    def second_copy(message, d):
        at, n, way = message
        first, second = places(way)
        ranks, number = pl.ds(at, n), numbers[message]
        return pltpu.make_async_remote_copy(
            second_out.at[d - 1, ranks], second_in.at[d - 1, ranks],
            second_send.at[number, d - 1], second_recv.at[number, d - 1],
            device_id={"term": term_at(way, first, lax.rem(second + d, side))}, device_id_type=MESH,
        )

    def give(message):
        at, n, way = message
        first, second = places(way)
        for rank in range(at, at + n):
            q = sector(rank)
            end = plan[ends, q]
            start = jnp.where(q > 0, plan[ends, jnp.maximum(q - 1, 0)], 0)
            for d in range(side):
                for b in range(side):
                    line = pl.multiple_of(term_at(way, lax.rem(first + d, side), b) * rows, rows)
                    total = running[jnp.maximum(end - 1, 0), pl.ds(line, rows), :]
                    total = jnp.where(end > start, total, jnp.zeros_like(total))
                    if d:
                        first_out[d - 1, rank, b] = total.astype(first_out.dtype)
                    else:
                        kept[rank, b] = total
        for d in range(1, side):
            first_copy(message, d).start()

    def pass_on(message):
        at, n, way = message
        first, second = places(way)
        for d in range(1, side):
            first_copy(message, d).wait_recv()
        for rank in range(at, at + n):
            for e in range(side):
                b = lax.rem(second + e, side)
                total = kept[rank, b]
                for d in range(1, side):
                    total = total + first_in[d - 1, rank, b].astype(jnp.float32)
                if e:
                    second_out[e - 1, rank] = total.astype(second_out.dtype)
                else:
                    own[rank] = total
        for e in range(1, side):
            second_copy(message, e).start()

    kept_row = lax.broadcasted_iota(jnp.int32, (rows, block), 0) + term * rows
    kept_col = lax.broadcasted_iota(jnp.int32, (rows, block), 1)
    kept_reach = jnp.maximum(kept_row, kept_col)

    def finish(message):
        at, n, way = message
        for d in range(1, side):
            second_copy(message, d).wait_recv()
        for rank in range(at, at + n):
            q = sector(rank)
            total = own[rank]
            for d in range(1, side):
                total = total + second_in[d - 1, rank].astype(jnp.float32)
            out_ref[q] = jnp.where(kept_reach < packed_scalars[0, 2 * slots + q], total, jnp.zeros_like(total))

    for stage, (start, count, messages) in enumerate(stages):
        receive(stage)
        if stage == 0:
            near_copy.wait_recv()
            left_load.wait()
            right_load.wait()
        compute(stage)
        for message in messages:
            give(message)
        if stage > 0:
            for i, message in enumerate(stages[stage - 1][2]):
                if SUMS[stage][i] is None:
                    pass_on(message)
    for message in stages[-1][2]:
        pass_on(message)
    for stage, (start, count, messages) in enumerate(stages):
        for message in messages:
            finish(message)

    near_copy.wait_send()

    @pl.when(has_far)
    def _():
        for i in range(len(arrivals)):
            far_copy(i, True).wait_send()
        for i in range(len(pairs)):
            pass_copy(i, True).wait_send()

    for message in numbers:
        for d in range(1, side):
            first_copy(message, d).wait_send()
            second_copy(message, d).wait_send()


def on_device(terms, groups, psi, sector_sizes, left_env, right_env, target, source, live_count):
    secs, block = psi.shape[0], psi.shape[1]
    slots = left_env.shape[0]
    rows, side = block // terms, math.isqrt(terms)
    stages = layout(secs)
    late = secs - stages[0][1]
    messages = sum(len(stage[2]) for stage in stages)
    passed = PARTS * sum(PAIRS)
    coming = secs - 2 * sum(PAIRS) + passed
    dma = pltpu.SemaphoreType.DMA
    here, vmem = pl.BlockSpec(memory_space=pl.ANY), pl.BlockSpec(memory_space=pltpu.VMEM)
    packed = jnp.concatenate(
        [target.reshape(1, slots), source.reshape(1, slots), sector_sizes.reshape(1, secs), live_count], axis=1
    )
    return pl.pallas_call(
        functools.partial(kernel, terms, groups),
        out_shape=jax.ShapeDtypeStruct((secs, rows, block), jnp.float32),
        in_specs=[vmem] + [here] * 3,
        out_specs=vmem,
        scratch_shapes=[
            pltpu.VMEM((3 * secs, block, block), jnp.bfloat16),
            pltpu.VMEM((late, block, block), jnp.bfloat16),
            pltpu.VMEM((slots, block, block), jnp.bfloat16),
            pltpu.VMEM((slots, block, block), jnp.bfloat16),
            pltpu.VMEM((slots, block, block), jnp.bfloat16),
            pltpu.VMEM((slots, block, block), jnp.float32),
            pltpu.VMEM((secs, side, rows, block), jnp.float32),
            pltpu.VMEM((secs, rows, block), jnp.float32),
            pltpu.VMEM((side - 1, secs, side, rows, block), jnp.bfloat16),
            pltpu.VMEM((side - 1, secs, side, rows, block), jnp.bfloat16),
            pltpu.VMEM((side - 1, secs, rows, block), jnp.bfloat16),
            pltpu.VMEM((side - 1, secs, rows, block), jnp.bfloat16),
            pltpu.SMEM((1, 2 * slots + secs + 1), jnp.int32),
            pltpu.VMEM((8, 128), jnp.int32),
            pltpu.SMEM((8, 128), jnp.int32),
            dma((9,)), dma, dma, dma((coming,)), dma((coming,)), dma((passed,)), dma((passed,)),
            *[dma((messages, side - 1))] * 4,
        ],
        compiler_params=pltpu.CompilerParams(
            collective_id=0, has_side_effects=True, vmem_limit_bytes=52 * 1024 * 1024
        ),
    )(
        packed,
        psi, left_env[:, 0], right_env[:, 0],
    )


def solution(mesh):
    placed = (
        P("sector", None, None),
        P("sector"),
        P("term", "sector", None, None),
        P("term", "sector", None, None),
        P("term", "sector"),
        P("term", "sector"),
        P("term", "sector"),
    )
    return jax.shard_map(
        functools.partial(on_device, mesh.shape["term"], mesh.shape["sector"]),
        mesh=mesh, in_specs=placed, out_specs=P("sector", "term", None), check_vma=False,
    )
```

```python
import functools
import math

import jax
import jax.numpy as jnp
from jax import lax
from jax.experimental import pallas as pl
from jax.experimental.pallas import tpu as pltpu
from jax.sharding import PartitionSpec as P

MESH = pl.DeviceIdType.MESH
SIXTEENTHS = (8, 8)
PARTS = 2
PAIRS = (3, 2)
HOOKS = ((), ((0, 16), (1, 0)))
SUMS = ((), ((1, 0), (1, 0), None, None))
SPLITS = ((2, 2, 2, 2), (3, 3, 1, 1))


def pieces(secs, shares):
    sizes = [secs * share // 16 for share in shares]
    return [(sum(sizes[:i]), size) for i, size in enumerate(sizes)]


def layout(secs):
    stages, start = [], 0
    for share, shares in zip(SIXTEENTHS, SPLITS):
        count = secs * share // 16
        messages = [(start + at, n, i % 2) for i, (at, n) in enumerate(pieces(secs, shares))]
        stages.append((start, count, messages))
        start += count
    return stages


def kernel(
    terms, groups,
    packed_ref, psi_ref, left_ref, right_ref,
    out_ref,
    pool, late, left, right, inner, running, kept, own, first_out, first_in, second_out, second_in,
    packed_scalars, table, plan,
    load_sems, near_send, near_recv, far_send, far_recv, pass_send, pass_recv,
    first_send, first_recv, second_send, second_recv,
):
    secs, block = psi_ref.shape[0], psi_ref.shape[1]
    slots = left_ref.shape[0]
    rows = block // terms
    side = math.isqrt(terms)
    stages = layout(secs)
    early = stages[0][1]
    group, term = lax.axis_index("sector"), lax.axis_index("term")
    odd = lax.rem(group, 2)
    near = group + 1 - 2 * odd
    far = group - 1 + 2 * odd
    has_far = jnp.logical_and(far >= 0, far < groups)
    col, row = lax.rem(term, side), lax.div(term, side)
    odd_col, odd_row = lax.rem(col, 2), lax.rem(row, 2)
    col_mate = term + 1 - 2 * odd_col
    row_mate = term + (1 - 2 * odd_row) * side
    mate = odd * row_mate + (1 - odd) * col_mate
    mine = odd * odd_row + (1 - odd) * odd_col
    mine_there = odd * odd_col + (1 - odd) * odd_row

    def sector(rank):
        return odd * rank + (1 - odd) * (secs - 1 - rank)

    half = secs // 2
    ahead, behind = odd * half, (1 - odd) * half

    def psi_load(at, sem):
        return pltpu.make_async_copy(psi_ref.at[pl.ds(at, half)], pool.at[pl.ds(at, half)], load_sems.at[sem])

    sizes_load = pltpu.make_async_copy(packed_ref, packed_scalars, load_sems.at[2])
    left_load = pltpu.make_async_copy(left_ref, left, load_sems.at[6])
    right_load = pltpu.make_async_copy(right_ref, right, load_sems.at[7])
    sizes_load.start()
    psi_load(ahead, 0).start()
    psi_load(behind, 1).start()

    barrier = pltpu.get_barrier_semaphore()
    pl.semaphore_signal(barrier, inc=1, device_id={"sector": near}, device_id_type=MESH)
    for d in range(1, side):
        for other in (row * side + lax.rem(col + d, side), lax.rem(row + d, side) * side + col):
            pl.semaphore_signal(barrier, inc=1, device_id={"term": other}, device_id_type=MESH)

    @pl.when(has_far)
    def _():
        pl.semaphore_signal(barrier, inc=1, device_id={"sector": far}, device_id_type=MESH)

    index_row = lax.broadcasted_iota(jnp.int32, (block, block), 0)
    index_col = lax.broadcasted_iota(jnp.int32, (block, block), 1)
    reach = jnp.maximum(index_row, index_col)

    def mask(at):
        def one(i, carry):
            q = at + i
            pool[q] = jnp.where(reach < packed_scalars[0, 2 * slots + q], pool[q], jnp.zeros((block, block), pool.dtype))
            return carry

        lax.fori_loop(0, half, one, 0, unroll=4)

    def landing(stage, rank):
        return pool.at[2 * secs + rank] if stage == 0 else late.at[rank - early]

    arrivals, pairs = [], []
    for stage, (start, count, messages) in enumerate(stages):
        paired = 2 * PAIRS[stage]
        for i in range(0, paired, 2):
            for part in range(PARTS):
                pairs.append((stage, start + i, part))
                arrivals.append((stage, start + i, part))
        arrivals.extend((stage, start + i, None) for i in range(paired, count))
    size = block // PARTS

    def part_of(ref, part):
        return ref if part is None else ref.at[pl.ds(part * size, size)]

    def far_copy(i, sending):
        stage, rank, part = arrivals[i]
        if part is not None:
            rank = rank + (mine_there if sending else mine)
        return pltpu.make_async_remote_copy(
            part_of(pool.at[secs - 1 - sector(rank)], part), part_of(landing(stage, rank), part),
            far_send.at[i], far_recv.at[i],
            device_id={"sector": far}, device_id_type=MESH,
        )

    def pass_copy(i, sending):
        stage, rank, part = pairs[i]
        at = part_of(landing(stage, rank + (mine if sending else 1 - mine)), part)
        return pltpu.make_async_remote_copy(
            at, at, pass_send.at[i], pass_recv.at[i], device_id={"term": mate}, device_id_type=MESH,
        )

    def arrival_of(pair):
        return arrivals.index(pairs[pair])

    near_copy = pltpu.make_async_remote_copy(
        pool.at[pl.ds(0, secs)], pool.at[pl.ds(secs, secs)], near_send, near_recv,
        device_id={"sector": near}, device_id_type=MESH,
    )

    sizes_load.wait()
    psi_load(ahead, 0).wait()
    left_load.start()
    mask(ahead)
    pl.semaphore_wait(barrier, 2 * side - 1 + has_far.astype(jnp.int32))

    @pl.when(has_far)
    def _():
        for i, (stage, rank, part) in enumerate(arrivals):
            if stage == 0:
                far_copy(i, True).start()

    psi_load(behind, 1).wait()
    right_load.start()
    mask(behind)

    @pl.when(has_far)
    def _():
        for i, (stage, rank, part) in enumerate(arrivals):
            if stage > 0:
                far_copy(i, True).start()

    near_copy.start()

    lane = lax.broadcasted_iota(jnp.int32, (slots, slots), 1)
    line = lax.broadcasted_iota(jnp.int32, (slots, slots), 0)
    slot = lax.broadcasted_iota(jnp.int32, (1, slots), 1)

    def as_column(values):
        return jnp.sum(jnp.where(lane == line, values, 0), axis=1, keepdims=True)

    tgt = jnp.where(slot < packed_scalars[0, 2 * slots + secs], packed_ref[:, 0:slots] - group * secs, secs)
    from_own = packed_ref[:, slots : 2 * slots] - group * secs
    from_near = packed_ref[:, slots : 2 * slots] - near * secs
    from_far = jnp.clip(packed_ref[:, slots : 2 * slots] - far * secs, 0, secs - 1)
    far_rank = odd * from_far + (1 - odd) * (secs - 1 - from_far)
    is_own = (from_own >= 0) & (from_own < secs)
    is_near = (from_near >= 0) & (from_near < secs)
    key = tgt * slots + slot
    order = jnp.sum((key < as_column(key)).astype(jnp.int32), axis=1, keepdims=True)
    table[...] = jnp.zeros_like(table)
    for stage, (start, count, messages) in enumerate(stages):
        ready = jnp.where(far_rank < start + count, 2 * secs + far_rank, 0)
        src = jnp.where(is_own, from_own, jnp.where(is_near, secs + from_near, ready))
        code = as_column(slot + src * 256 + tgt * 65536)
        table[stage : stage + 1, 0:slots] = jnp.sum(jnp.where(order == lane, code, 0), axis=0, keepdims=True)
    sec = lax.broadcasted_iota(jnp.int32, (slots, 128), 1)
    ends = len(stages)
    table[ends : ends + 1, :] = jnp.sum((as_column(tgt) <= sec).astype(jnp.int32), axis=0, keepdims=True)
    plan_load = pltpu.make_async_copy(table, plan, load_sems.at[8])
    plan_load.start()
    plan_load.wait()

    def forward(pair):
        @pl.when(has_far)
        def _():
            for i in range(PARTS * pair, PARTS * (pair + 1)):
                far_copy(arrival_of(i), False).wait_recv()
                pass_copy(i, True).start()

    def hooks(stage, loop, k):
        if stage + 1 < len(stages):
            for i, hook in enumerate(HOOKS[stage + 1]):
                if hook == (loop, k):
                    forward(sum(PAIRS[: stage + 1]) + i)
        if stage > 0:
            for i, hook in enumerate(SUMS[stage]):
                if hook == (loop, k):
                    pass_on(stages[stage - 1][2][i])

    def receive(stage):
        start, count, messages = stages[stage]
        for i in range(PAIRS[stage]):
            if stage == 0 or HOOKS[stage][i] is None:
                forward(sum(PAIRS[:stage]) + i)

        @pl.when(has_far)
        def _():
            for i, (at, rank, part) in enumerate(arrivals):
                if at == stage and part is None:
                    far_copy(i, False).wait_recv()
            for i, (at, rank, part) in enumerate(pairs):
                if at == stage:
                    pass_copy(i, False).wait_recv()
            if stage > 0:
                for i in range(count):
                    pool[2 * secs + start + i] = late[start + i - early]

    def compute(stage):
        for k in range(slots):
            hooks(stage, 0, k)
            code = plan[stage, k]
            inner[k] = jnp.dot(
                left[code & 255], pool[(code >> 8) & 255], preferred_element_type=jnp.float32
            ).astype(jnp.bfloat16)
        total, before = jnp.zeros((block, block), jnp.float32), secs
        for k in range(slots):
            hooks(stage, 1, k)
            code = plan[stage, k]
            tgt = code >> 16
            here = lax.dot_general(
                inner[k], right[code & 255], (((1,), (1,)), ((), ())), preferred_element_type=jnp.float32
            )
            total = here + jnp.where(tgt == before, total, jnp.zeros_like(total)) if k else here
            running[k] = total
            before = tgt
        hooks(stage, 2, 0)

    def places(way):
        return (row, col) if way else (col, row)

    def term_at(way, first, second):
        return first * side + second if way else second * side + first

    numbers = {}
    for stage, (start, count, messages) in enumerate(stages):
        for message in messages:
            numbers[message] = len(numbers)

    def first_copy(message, d):
        at, n, way = message
        first, second = places(way)
        ranks, number = pl.ds(at, n), numbers[message]
        return pltpu.make_async_remote_copy(
            first_out.at[d - 1, ranks], first_in.at[d - 1, ranks],
            first_send.at[number, d - 1], first_recv.at[number, d - 1],
            device_id={"term": term_at(way, lax.rem(first + d, side), second)}, device_id_type=MESH,
        )

    def second_copy(message, d):
        at, n, way = message
        first, second = places(way)
        ranks, number = pl.ds(at, n), numbers[message]
        return pltpu.make_async_remote_copy(
            second_out.at[d - 1, ranks], second_in.at[d - 1, ranks],
            second_send.at[number, d - 1], second_recv.at[number, d - 1],
            device_id={"term": term_at(way, first, lax.rem(second + d, side))}, device_id_type=MESH,
        )

    def give(message):
        at, n, way = message
        first, second = places(way)
        for rank in range(at, at + n):
            q = sector(rank)
            end = plan[ends, q]
            start = jnp.where(q > 0, plan[ends, jnp.maximum(q - 1, 0)], 0)
            for d in range(side):
                for b in range(side):
                    line = pl.multiple_of(term_at(way, lax.rem(first + d, side), b) * rows, rows)
                    total = running[jnp.maximum(end - 1, 0), pl.ds(line, rows), :]
                    total = jnp.where(end > start, total, jnp.zeros_like(total))
                    if d:
                        first_out[d - 1, rank, b] = total.astype(first_out.dtype)
                    else:
                        kept[rank, b] = total
        for d in range(1, side):
            first_copy(message, d).start()

    def pass_on(message):
        at, n, way = message
        first, second = places(way)
        for d in range(1, side):
            first_copy(message, d).wait_recv()
        for rank in range(at, at + n):
            for e in range(side):
                b = lax.rem(second + e, side)
                total = kept[rank, b]
                for d in range(1, side):
                    total = total + first_in[d - 1, rank, b].astype(jnp.float32)
                if e:
                    second_out[e - 1, rank] = total.astype(second_out.dtype)
                else:
                    own[rank] = total
        for e in range(1, side):
            second_copy(message, e).start()

    kept_row = lax.broadcasted_iota(jnp.int32, (rows, block), 0) + term * rows
    kept_col = lax.broadcasted_iota(jnp.int32, (rows, block), 1)
    kept_reach = jnp.maximum(kept_row, kept_col)

    def finish(message):
        at, n, way = message
        for d in range(1, side):
            second_copy(message, d).wait_recv()
        for rank in range(at, at + n):
            q = sector(rank)
            total = own[rank]
            for d in range(1, side):
                total = total + second_in[d - 1, rank].astype(jnp.float32)
            out_ref[q] = jnp.where(kept_reach < packed_scalars[0, 2 * slots + q], total, jnp.zeros_like(total))

    for stage, (start, count, messages) in enumerate(stages):
        receive(stage)
        if stage == 0:
            near_copy.wait_recv()
            left_load.wait()
            right_load.wait()
        compute(stage)
        for message in messages:
            give(message)
        if stage > 0:
            for i, message in enumerate(stages[stage - 1][2]):
                if SUMS[stage][i] is None:
                    pass_on(message)
    for message in stages[-1][2]:
        pass_on(message)
    for stage, (start, count, messages) in enumerate(stages):
        for message in messages:
            finish(message)

    near_copy.wait_send()

    @pl.when(has_far)
    def _():
        for i in range(len(arrivals)):
            far_copy(i, True).wait_send()
        for i in range(len(pairs)):
            pass_copy(i, True).wait_send()

    for message in numbers:
        for d in range(1, side):
            first_copy(message, d).wait_send()
            second_copy(message, d).wait_send()


def on_device(terms, groups, psi, sector_sizes, left_env, right_env, target, source, live_count):
    secs, block = psi.shape[0], psi.shape[1]
    slots = left_env.shape[0]
    rows, side = block // terms, math.isqrt(terms)
    stages = layout(secs)
    late = secs - stages[0][1]
    messages = sum(len(stage[2]) for stage in stages)
    passed = PARTS * sum(PAIRS)
    coming = secs - 2 * sum(PAIRS) + passed
    dma = pltpu.SemaphoreType.DMA
    here, vmem = pl.BlockSpec(memory_space=pl.ANY), pl.BlockSpec(memory_space=pltpu.VMEM)
    packed = jnp.concatenate(
        [target.reshape(1, slots), source.reshape(1, slots), sector_sizes.reshape(1, secs), live_count], axis=1
    )
    return pl.pallas_call(
        functools.partial(kernel, terms, groups),
        out_shape=jax.ShapeDtypeStruct((secs, rows, block), jnp.float32),
        in_specs=[vmem] + [here] * 3,
        out_specs=vmem,
        scratch_shapes=[
            pltpu.VMEM((3 * secs, block, block), jnp.bfloat16),
            pltpu.VMEM((late, block, block), jnp.bfloat16),
            pltpu.VMEM((slots, block, block), jnp.bfloat16),
            pltpu.VMEM((slots, block, block), jnp.bfloat16),
            pltpu.VMEM((slots, block, block), jnp.bfloat16),
            pltpu.VMEM((slots, block, block), jnp.float32),
            pltpu.VMEM((secs, side, rows, block), jnp.float32),
            pltpu.VMEM((secs, rows, block), jnp.float32),
            pltpu.VMEM((side - 1, secs, side, rows, block), jnp.bfloat16),
            pltpu.VMEM((side - 1, secs, side, rows, block), jnp.bfloat16),
            pltpu.VMEM((side - 1, secs, rows, block), jnp.bfloat16),
            pltpu.VMEM((side - 1, secs, rows, block), jnp.bfloat16),
            pltpu.SMEM((1, 2 * slots + secs + 1), jnp.int32),
            pltpu.VMEM((8, 128), jnp.int32),
            pltpu.SMEM((8, 128), jnp.int32),
            dma((9,)), dma, dma, dma((coming,)), dma((coming,)), dma((passed,)), dma((passed,)),
            *[dma((messages, side - 1))] * 4,
        ],
        compiler_params=pltpu.CompilerParams(
            collective_id=0, has_side_effects=True, vmem_limit_bytes=52 * 1024 * 1024
        ),
    )(
        packed,
        psi, left_env[:, 0], right_env[:, 0],
    )


def solution(mesh):
    placed = (
        P("sector", None, None),
        P("sector"),
        P("term", "sector", None, None),
        P("term", "sector", None, None),
        P("term", "sector"),
        P("term", "sector"),
        P("term", "sector"),
    )
    return jax.shard_map(
        functools.partial(on_device, mesh.shape["term"], mesh.shape["sector"]),
        mesh=mesh, in_specs=placed, out_specs=P("sector", "term", None), check_vma=False,
    )
```
